32 devices in a mesh: replica: 4 (over y, x), fsdp: 2 (over core), tensor: 4 (over z).
Axes of the slice: x: 2, y: 2, z: 4, core: 2. Of those that a mesh axis runs over, the one named last changes fastest.
Arguments:
- attn_out: bfloat16 [2048, 8192], P(('replica', 'tensor'), 'fsdp'), may hold values from -6 to 6
- out_grad: bfloat16 [2048, 8192], P(('replica', 'fsdp'), 'tensor'), may hold values from -0.25 to 0.25
- error_in: float32 [4, 8192, 8192], P('replica', 'fsdp', 'tensor'), may hold values from -4 to 4
- factor_in: float32 [8192, 32], P('tensor'), may hold values from -0.0625 to 0.0625
Outputs:
- new_error: float32 [4, 8192, 8192], P('replica', 'fsdp', 'tensor')
- update: bfloat16 [8192, 8192], P('fsdp', 'tensor')
- new_factor: float32 [8192, 32], P('tensor')
The draws below stay inside these ranges and needn't reach their ends.
All inputs are finite; a program needn't handle non-finite values.
Results may differ from the reference program's by a relative error of at most 0.001.
Values may be sent and summed in bfloat16 or wider, within the bound.
A program may use at most 128 MiB of HBM per device.

```python
import jax
import jax.numpy as jnp
from jax import lax

DIN = 8192
DOUT = 8192
RANK = 32
TOK = 512
TOK_ALL = 2048
N_REPLICA = 4


def shard_levels(own_key, shape, cuts, least, high):
    factor_of, own = 1.0, jax.random.fold_in(own_key, 6)
    for axis_at, parts in cuts:
        steps = jnp.exp(jax.random.uniform(jax.random.fold_in(own, axis_at), (parts,), jnp.float32, least / len(cuts), high / len(cuts)))
        factor_of = factor_of * jnp.repeat(steps, shape[axis_at] // parts).reshape([-1 if axis == axis_at else 1 for axis in range(len(shape))])
    return factor_of


def centred(rng, extent, deviation, reach, cuts=(), kind=jnp.bfloat16):
    drawn = jax.random.normal(rng, extent, jnp.float32) * deviation
    if len(cuts) > 0:
        drawn = shard_levels(rng, extent, cuts, -0.22, 0.18) * drawn
    return jnp.clip(drawn, min=-reach, max=reach).astype(kind)


def setup_inputs(seed: int = 0) -> dict:
    arg_keys = jax.random.split(jax.random.key(seed), 5)
    return {
        "attn_out": centred(arg_keys[0], (TOK_ALL, DIN), 1.0, 6.0, ((0, 16), (1, 2))),
        "out_grad": centred(arg_keys[1], (TOK_ALL, DOUT), TOK ** -0.5, 0.25, ((0, 8), (1, 4))),
        "error_in": centred(arg_keys[2], (N_REPLICA, DIN, DOUT), 0.5, 4.0, ((0, 4), (1, 2), (2, 4)), jnp.float32),
        "factor_in": centred(arg_keys[3], (DOUT, RANK), DOUT ** -0.5, 0.0625, ((0, 4),), jnp.float32),
    }


def reference(attn_out, out_grad, error_in, factor_in):
    tokens = attn_out.shape[0] // N_REPLICA
    activations = attn_out.reshape(N_REPLICA, tokens, DIN)
    cotangents = out_grad.reshape(N_REPLICA, tokens, DOUT)

    def per_replica(items):
        act_block, cot_block, memory = items
        return jnp.dot(act_block.T.astype(jnp.float32), cot_block.astype(jnp.float32), preferred_element_type=jnp.float32) + memory
    merged = lax.map(per_replica, (activations, cotangents, error_in))
    left = jnp.einsum('rij,jk->ik', merged, factor_in, precision=lax.Precision.HIGHEST) / N_REPLICA
    gram_matrix = jnp.dot(left.T, left, precision=lax.Precision.HIGHEST)
    triangle = jnp.linalg.cholesky(gram_matrix)
    orthonormal = jax.scipy.linalg.solve_triangular(triangle, left.T, lower=True).T
    new_factor = jnp.einsum('rij,ik->jk', merged, orthonormal, precision=lax.Precision.HIGHEST) / N_REPLICA
    decompressed = jnp.dot(orthonormal, new_factor.T, precision=lax.Precision.HIGHEST)
    new_error = merged - decompressed[None]
    return (new_error, decompressed.astype(jnp.bfloat16), new_factor)
```

```python
import functools

import jax
import jax.numpy as jnp
from jax import lax
from jax.experimental import pallas as pl
from jax.experimental.pallas import tpu as pltpu
from jax.sharding import PartitionSpec as P

MESH = pl.DeviceIdType.MESH
HIGHEST = lax.Precision.HIGHEST
F32, BF16 = jnp.float32, jnp.bfloat16
LANE = 128
NN = (((1,), (0,)), ((), ()))
NT = (((1,), (1,)), ((), ()))
TN = (((0,), (0,)), ((), ()))
VMEM_BYTES = 60 * 1024 * 1024


def mul(a, b, dims=NN, precision=None):
    return lax.dot_general(a, b, dims, precision=precision, preferred_element_type=F32)


def split(x):
    high = x.astype(BF16)
    return high, (x - high.astype(F32)).astype(BF16)


def stacked(x):
    return jnp.concatenate(split(x), axis=0)


def folded(x):
    half = x.shape[0] // 2
    return x[:half] + x[half:]


class Cut:
    def __init__(self, rows, columns, pieces):
        self.down = 1
        while (columns * self.down) % (pieces * LANE) != 0:
            self.down *= 2
        self.across = pieces // self.down
        self.rows, self.columns = rows // self.down, columns // self.across

    def at(self, piece, start=0):
        row = pl.multiple_of((piece // self.across) * self.rows, 8)
        column = pl.multiple_of(start + (piece % self.across) * self.columns, LANE)
        return pl.ds(row, self.rows), pl.ds(column, self.columns)


def inverse_factor(gram):
    rank = gram.shape[0]
    row_at = lax.broadcasted_iota(jnp.int32, (rank, LANE), 0)
    lane_at = lax.broadcasted_iota(jnp.int32, (rank, LANE), 1)
    table = gram + jnp.where(lane_at == row_at + LANE // 2, 1.0, 0.0).astype(F32)
    for k in range(rank):
        row = table[k : k + 1, :]
        inverse = 1.0 / jnp.sqrt(row[:, k : k + 1])
        row = row * inverse
        column = jnp.where(row_at > k, table[:, k : k + 1] * inverse, 0.0)
        table = jnp.where(row_at == k, jnp.broadcast_to(row, table.shape), table - column * row)
    return table[:, LANE // 2 : LANE // 2 + rank]


def front(
    sizes,
    a_ref, g_ref, f_ref, e_ref,
    q_ref, n_ref, nt_ref,
    e_mem, f_mem, part, left, got_rep, mid, got_ten, gf_slots, gf_all, mix_slots, al_all,
    n_part, n_got, n_full,
    e_sem, gf_sem, rep_sem, ten_sem, ten_back, rep_back, mix_sem, n_sem, n_back,
):
    reps, fs, ts = sizes
    r, f, t = lax.axis_index("replica"), lax.axis_index("fsdp"), lax.axis_index("tensor")
    rank, rows = part.shape
    block = rows // reps
    tile = min(256, block)
    per = block // tile
    tok_g, tok_a = g_ref.shape[0], a_ref.shape[0]

    def row_copy(step):
        q = lax.rem(r + 1 + step // per, reps)
        at = pl.ds(pl.multiple_of(q * block + (step % per) * tile, tile), tile)
        return pltpu.make_async_copy(e_ref.at[at], e_mem.at[at], e_sem.at[step])

    for step in range(reps * per):
        row_copy(step).start()

    plane = [(df, dt) for df in range(fs) for dt in range(ts) if df + dt > 0]
    sheet = [(dr, df) for dr in range(reps) for df in range(fs) if dr + df > 0]

    def in_plane(df, dt):
        return {"replica": r, "fsdp": lax.rem(f + df, fs), "tensor": lax.rem(t + dt, ts)}

    def in_sheet(dr, df):
        return {"replica": lax.rem(r + dr, reps), "fsdp": lax.rem(f + df, fs), "tensor": t}

    barrier = pltpu.get_barrier_semaphore()
    greeted = [in_plane(*d) for d in plane] + [in_sheet(*d) for d in sheet if d[0] > 0]
    for device in greeted:
        pl.semaphore_signal(barrier, inc=1, device_id=device, device_id_type=MESH)

    high, low = split(f_ref[...])
    f_mem[...] = jnp.zeros(f_mem.shape, BF16)
    f_mem[:, 0:rank] = high
    f_mem[:, LANE : LANE + rank] = low

    me_plane = f * ts + t
    projected = mul(g_ref[...], f_mem[...])
    projected = (projected[:, :LANE] + projected[:, LANE:]).T[:rank]
    gf_slots[me_plane] = projected
    pl.semaphore_wait(barrier, len(greeted))

    def spread(slots, sems):
        copies = []
        for i, d in enumerate(plane):
            copies.append(pltpu.make_async_remote_copy(
                src_ref=slots.at[me_plane], dst_ref=slots.at[me_plane],
                send_sem=sems.at[0, i], recv_sem=sems.at[1, i],
                device_id=in_plane(*d), device_id_type=MESH,
            ))
            copies[-1].start()
        return copies

    gf_copies = spread(gf_slots, gf_sem)

    rep_copies = []
    for dr in range(1, reps + 1):
        q = lax.rem(r + dr, reps)
        base = pl.multiple_of(q * block, LANE)

        def tile_left(j, _, dr=dr, base=base):
            row_copy((dr - 1) * per + j).wait()
            at = pl.ds(pl.multiple_of(base + j * tile, tile), tile)
            eh, el = split(e_mem[at, :])
            wide = mul(eh, f_mem[...])
            total = wide[:, :LANE] + wide[:, LANE:] + mul(el, f_mem[:, :LANE])
            part[:, at] = total.T[:rank]
            return 0

        lax.fori_loop(0, per, tile_left, 0)
        if dr == 1:
            for copy in gf_copies:
                copy.wait()
            for df in range(fs):
                total = gf_slots[df * ts]
                for dt in range(1, ts):
                    total = total + gf_slots[df * ts + dt]
                gf_all[:, df * tok_g : (df + 1) * tok_g] = total
        own = stacked(gf_all[:, pl.ds(pl.multiple_of(t * tok_a, LANE), tok_a)])
        at = pl.ds(base, block)
        part[:, at] += folded(mul(own, a_ref[:, at]))
        if dr < reps:
            copy = pltpu.make_async_remote_copy(
                src_ref=part.at[:, at], dst_ref=got_rep.at[dr - 1],
                send_sem=rep_sem.at[0, dr - 1], recv_sem=rep_sem.at[1, dr - 1],
                device_id=in_sheet(dr, 0), device_id_type=MESH,
            )
            copy.start()
            rep_copies.append(copy)

    mine = pl.ds(pl.multiple_of(r * block, LANE), block)
    total = part[:, mine]
    for i, copy in enumerate(rep_copies):
        copy.wait()
        total = total + got_rep[i]
    mid[...] = total

    cut = Cut(rank, block, ts)
    ten_copies = []
    for dt in range(1, ts):
        copy = pltpu.make_async_remote_copy(
            src_ref=mid.at[cut.at(lax.rem(t + dt, ts))], dst_ref=got_ten.at[dt - 1],
            send_sem=ten_sem.at[0, dt - 1], recv_sem=ten_sem.at[1, dt - 1],
            device_id=in_plane(0, dt), device_id_type=MESH,
        )
        copy.start()
        ten_copies.append(copy)
    total = mid[cut.at(t)]
    for i, copy in enumerate(ten_copies):
        copy.wait()
        total = total + got_ten[i]
    own = cut.at(t, r * block)
    left[own] = total * (1.0 / reps)
    back = []
    for dt in range(1, ts):
        copy = pltpu.make_async_remote_copy(
            src_ref=left.at[own], dst_ref=left.at[own],
            send_sem=ten_back.at[0, dt - 1], recv_sem=ten_back.at[1, dt - 1],
            device_id=in_plane(0, dt), device_id_type=MESH,
        )
        copy.start()
        back.append(copy)
    for copy in back:
        copy.wait()
    back = []
    for dr in range(1, reps):
        copy = pltpu.make_async_remote_copy(
            src_ref=left.at[:, mine], dst_ref=left.at[:, mine],
            send_sem=rep_back.at[0, dr - 1], recv_sem=rep_back.at[1, dr - 1],
            device_id=in_sheet(dr, 0), device_id_type=MESH,
        )
        copy.start()
        back.append(copy)
    for copy in back:
        copy.wait()

    whole = left[...]
    mix_slots[me_plane, :, 0:LANE] = jnp.zeros((rank, LANE), F32)
    mix_slots[me_plane, :, 0:rank] = mul(whole, whole, NT, HIGHEST)
    mix_slots[me_plane, :, LANE:] = folded(mul(stacked(whole), a_ref[...], NT))
    mix_copies = spread(mix_slots, mix_sem)

    n_part[...] = jnp.zeros(n_part.shape, F32)

    def tile_right(j, _):
        at = pl.ds(pl.multiple_of(j * tile, tile), tile)
        eh, el = split(e_mem[at, :])
        both = stacked(left[:, at])
        n_part[...] += folded(mul(both, eh)) + mul(both[:rank], el)
        return 0

    lax.fori_loop(0, rows // tile, tile_right, 0)

    for copy in mix_copies:
        copy.wait()
    for dt in range(ts):
        total = mix_slots[dt, :, LANE:]
        for df in range(1, fs):
            total = total + mix_slots[df * ts + dt, :, LANE:]
        al_all[:, dt * tok_a : (dt + 1) * tok_a] = total
    tokens = stacked(al_all[:, pl.ds(pl.multiple_of(f * tok_g, LANE), tok_g)])
    n_part[...] += folded(mul(tokens, g_ref[...]))

    n_cut = Cut(rank, n_part.shape[1], reps * fs)
    n_copies = []
    for i, (dr, df) in enumerate(sheet):
        owner = lax.rem(r + dr, reps) * fs + lax.rem(f + df, fs)
        copy = pltpu.make_async_remote_copy(
            src_ref=n_part.at[n_cut.at(owner)], dst_ref=n_got.at[i],
            send_sem=n_sem.at[0, i], recv_sem=n_sem.at[1, i],
            device_id=in_sheet(dr, df), device_id_type=MESH,
        )
        copy.start()
        n_copies.append(copy)

    gram = mix_slots[0, :, 0:LANE]
    for df in range(1, fs):
        gram = gram + mix_slots[df * ts, :, 0:LANE]
    inverse = inverse_factor(gram)
    high, low = split(mul(inverse, left[...], precision=HIGHEST))
    q_ref[0:rank] = high
    q_ref[rank : 2 * rank] = low
    q_ref[2 * rank :] = high

    place = n_cut.at(r * fs + f)
    total = n_part[place]
    for i, copy in enumerate(n_copies):
        copy.wait()
        total = total + n_got[i]
    n_full[place] = total * (1.0 / reps)
    back = []
    for i, (dr, df) in enumerate(sheet):
        copy = pltpu.make_async_remote_copy(
            src_ref=n_full.at[place], dst_ref=n_full.at[place],
            send_sem=n_back.at[0, i], recv_sem=n_back.at[1, i],
            device_id=in_sheet(dr, df), device_id_type=MESH,
        )
        copy.start()
        back.append(copy)
    for copy in back:
        copy.wait()
    factor = mul(inverse, n_full[...], precision=HIGHEST)
    n_ref[...] = factor
    high, low = split(factor)
    nt_ref[0:rank] = high
    nt_ref[rank : 2 * rank] = high
    nt_ref[2 * rank :] = low


def run_front(sizes, a, g, f, e):
    reps, fs, ts = sizes
    rank, rows, columns = f.shape[1], e.shape[0], e.shape[1]
    tok_g, tok_a = g.shape[0], a.shape[0]
    block = rows // reps
    cut, n_cut = Cut(rank, block, ts), Cut(rank, columns, reps * fs)
    tiles = rows // min(256, block)
    plane, sheet = fs * ts - 1, reps * fs - 1
    vmem = pl.BlockSpec(memory_space=pltpu.VMEM)
    dma = pltpu.SemaphoreType.DMA
    return pl.pallas_call(
        functools.partial(front, sizes),
        out_shape=(
            jax.ShapeDtypeStruct((3 * rank, rows), BF16),
            jax.ShapeDtypeStruct((rank, columns), F32),
            jax.ShapeDtypeStruct((3 * rank, columns), BF16),
        ),
        in_specs=[vmem, vmem, vmem, pl.BlockSpec(memory_space=pl.ANY)],
        out_specs=(vmem, vmem, vmem),
        scratch_shapes=[
            pltpu.VMEM((rows, columns), F32),
            pltpu.VMEM((columns, 2 * LANE), BF16),
            pltpu.VMEM((rank, rows), F32),
            pltpu.VMEM((rank, rows), F32),
            pltpu.VMEM((reps - 1, rank, block), F32),
            pltpu.VMEM((rank, block), F32),
            pltpu.VMEM((ts - 1, cut.rows, cut.columns), F32),
            pltpu.VMEM((fs * ts, rank, tok_g), F32),
            pltpu.VMEM((rank, tok_g * fs), F32),
            pltpu.VMEM((fs * ts, rank, LANE + tok_a), F32),
            pltpu.VMEM((rank, tok_a * ts), F32),
            pltpu.VMEM((rank, columns), F32),
            pltpu.VMEM((sheet, n_cut.rows, n_cut.columns), F32),
            pltpu.VMEM((rank, columns), F32),
            dma((tiles,)), dma((2, plane)), dma((2, reps - 1)), dma((2, ts - 1)), dma((2, ts - 1)),
            dma((2, reps - 1)), dma((2, plane)), dma((2, sheet)), dma((2, sheet)),
        ],
        compiler_params=pltpu.CompilerParams(
            collective_id=0, has_side_effects=True, vmem_limit_bytes=VMEM_BYTES
        ),
        cost_estimate=pl.CostEstimate(
            flops=100_000_000_000, bytes_accessed=rows * columns * 8, transcendentals=0
        ),
        name="front",
    )(a, g, f, e)


def finish(a_ref, g_ref, e_ref, q_ref, n_ref, error_ref, update_ref):
    low_rank = mul(q_ref[...], n_ref[...], TN)
    grad = mul(a_ref[...], g_ref[...], TN)
    error_ref[...] = grad + e_ref[...] - low_rank
    update_ref[...] = low_rank.astype(BF16)


def run_finish(a, g, e, q, n):
    rows, columns = e.shape
    tile = min(256, rows)

    def whole(x):
        return pl.BlockSpec(x.shape, lambda i: (0, 0))

    def tall(x):
        return pl.BlockSpec((x.shape[0], tile), lambda i: (0, i))

    flat = pl.BlockSpec((tile, columns), lambda i: (i, 0))
    return pl.pallas_call(
        finish,
        out_shape=(jax.ShapeDtypeStruct(e.shape, F32), jax.ShapeDtypeStruct(e.shape, BF16)),
        grid=(rows // tile,),
        in_specs=[tall(a), whole(g), flat, tall(q), whole(n)],
        out_specs=(flat, flat),
        compiler_params=pltpu.CompilerParams(vmem_limit_bytes=VMEM_BYTES),
        name="finish",
    )(a, g, e, q, n)


def solution(mesh):
    sizes = (mesh.shape["replica"], mesh.shape["fsdp"], mesh.shape["tensor"])

    def body(attn_out, out_grad, error_in, factor_in):
        memory = error_in[0]
        activations = lax.all_gather(attn_out, "tensor", axis=0, tiled=True)
        cotangents = lax.all_gather(out_grad, "fsdp", axis=0, tiled=True)
        q, factor, n = run_front(sizes, attn_out, out_grad, factor_in, memory)
        new_error, update = run_finish(activations, cotangents, memory, q, n)
        return new_error[None], update, factor.T

    placed = (
        P(("replica", "tensor"), "fsdp"),
        P(("replica", "fsdp"), "tensor"),
        P("replica", "fsdp", "tensor"),
        P("tensor", None),
    )
    return jax.shard_map(
        body,
        mesh=mesh,
        in_specs=placed,
        out_specs=(P("replica", "fsdp", "tensor"), P("fsdp", "tensor"), P("tensor", None)),
        check_vma=False,
    )
```

```python
import functools

import jax
import jax.numpy as jnp
from jax import lax
from jax.experimental import pallas as pl
from jax.experimental.pallas import tpu as pltpu
from jax.sharding import PartitionSpec as P

MESH = pl.DeviceIdType.MESH
HIGHEST = lax.Precision.HIGHEST
F32, BF16 = jnp.float32, jnp.bfloat16
LANE = 128
NN = (((1,), (0,)), ((), ()))
NT = (((1,), (1,)), ((), ()))
TN = (((0,), (0,)), ((), ()))
VMEM_BYTES = 20 * 1024 * 1024


def mul(a, b, dims=NN, precision=None):
    return lax.dot_general(a, b, dims, precision=precision, preferred_element_type=F32)


def split(x):
    high = x.astype(BF16)
    return high, (x - high.astype(F32)).astype(BF16)


def stacked(x):
    return jnp.concatenate(split(x), axis=0)


def folded(x):
    half = x.shape[0] // 2
    return x[:half] + x[half:]


class Cut:
    def __init__(self, rows, columns, pieces):
        self.down = 1
        while (columns * self.down) % (pieces * LANE) != 0:
            self.down *= 2
        self.across = pieces // self.down
        self.rows, self.columns = rows // self.down, columns // self.across

    def at(self, piece, start=0):
        row = pl.multiple_of((piece // self.across) * self.rows, 8)
        column = pl.multiple_of(start + (piece % self.across) * self.columns, LANE)
        return pl.ds(row, self.rows), pl.ds(column, self.columns)


def inverse_factor(gram):
    rank = gram.shape[0]
    row_at = lax.broadcasted_iota(jnp.int32, (rank, LANE), 0)
    lane_at = lax.broadcasted_iota(jnp.int32, (rank, LANE), 1)
    table = gram + jnp.where(lane_at == row_at + LANE // 2, 1.0, 0.0).astype(F32)
    for k in range(rank):
        row = table[k : k + 1, :]
        inverse = 1.0 / jnp.sqrt(row[:, k : k + 1])
        row = row * inverse
        column = jnp.where(row_at > k, table[:, k : k + 1] * inverse, 0.0)
        table = jnp.where(row_at == k, jnp.broadcast_to(row, table.shape), table - column * row)
    return table[:, LANE // 2 : LANE // 2 + rank]


def front(
    sizes,
    a_ref, g_ref, f_ref, e_ref,
    q_ref, n_ref, nt_ref, e_mem, a_all, g_all,
    f_mem, part, left, got_rep, mid, got_ten, gf_slots, gf_all, mix_slots, al_all,
    n_part, n_got, n_full,
    e_sem, own_sem, ring_sem, g_sem, gf_sem, rep_sem, ten_sem, ten_back, rep_back, mix_sem, n_sem, n_back,
):
    reps, fs, ts = sizes
    r, f, t = lax.axis_index("replica"), lax.axis_index("fsdp"), lax.axis_index("tensor")
    rank, rows = part.shape
    block = rows // reps
    tile = min(256, block)
    per = block // tile
    tok_g, tok_a = g_ref.shape[0], a_ref.shape[0]

    def row_copy(step):
        q = lax.rem(r + 1 + step // per, reps)
        at = pl.ds(pl.multiple_of(q * block + (step % per) * tile, tile), tile)
        return pltpu.make_async_copy(e_ref.at[at], e_mem.at[at], e_sem.at[step])

    for step in range(reps * per):
        row_copy(step).start()

    plane = [(df, dt) for df in range(fs) for dt in range(ts) if df + dt > 0]
    sheet = [(dr, df) for dr in range(reps) for df in range(fs) if dr + df > 0]

    def in_plane(df, dt):
        return {"replica": r, "fsdp": lax.rem(f + df, fs), "tensor": lax.rem(t + dt, ts)}

    def in_sheet(dr, df):
        return {"replica": lax.rem(r + dr, reps), "fsdp": lax.rem(f + df, fs), "tensor": t}

    barrier = pltpu.get_barrier_semaphore()
    greeted = [in_plane(*d) for d in plane] + [in_sheet(*d) for d in sheet if d[0] > 0]
    for device in greeted:
        pl.semaphore_signal(barrier, inc=1, device_id=device, device_id_type=MESH)

    high, low = split(f_ref[...])
    wide = jnp.concatenate(
        [high.astype(F32), low.astype(F32), jnp.zeros((LANE - 2 * rank, f_ref.shape[1]), F32)], axis=0
    )
    f_mem[...] = wide.T.astype(BF16)

    me_plane = f * ts + t
    gf_slots[me_plane] = folded(mul(g_ref[...], f_mem[...]).T[: 2 * rank])
    pl.semaphore_wait(barrier, len(greeted))

    def spread(slots, sems):
        copies = []
        for i, d in enumerate(plane):
            copies.append(pltpu.make_async_remote_copy(
                src_ref=slots.at[me_plane], dst_ref=slots.at[me_plane],
                send_sem=sems.at[0, i], recv_sem=sems.at[1, i],
                device_id=in_plane(*d), device_id_type=MESH,
            ))
            copies[-1].start()
        return copies

    gf_copies = spread(gf_slots, gf_sem)

    g_own = pl.ds(pl.multiple_of(f * tok_g, tok_g), tok_g)
    a_own = pl.ds(pl.multiple_of(t * tok_a, tok_a), tok_a)
    own_copies = [
        pltpu.make_async_copy(a_ref, a_all.at[a_own], own_sem.at[0]),
        pltpu.make_async_copy(g_ref, g_all.at[g_own], own_sem.at[1]),
    ]
    for copy in own_copies:
        copy.start()
    g_copies = []
    for df in range(1, fs):
        copy = pltpu.make_async_remote_copy(
            src_ref=g_ref, dst_ref=g_all.at[g_own],
            send_sem=g_sem.at[0, df - 1], recv_sem=g_sem.at[1, df - 1],
            device_id=in_plane(df, 0), device_id_type=MESH,
        )
        copy.start()
        g_copies.append(copy)

    half = tok_a // 2

    def ring_copy(step, way, part_at):
        block_at = lax.rem(t - step + ts, ts) if way == 0 else lax.rem(t + step, ts)
        upper = (part_at == 0) == (way == 0)
        first = 0 if upper else half
        rows_at = pl.ds(pl.multiple_of(block_at * tok_a + first, half), half)
        src = a_ref.at[pl.ds(first, half)] if step == 0 else a_all.at[rows_at]
        slot = (step * 2 + way) * 2 + part_at
        return pltpu.make_async_remote_copy(
            src_ref=src, dst_ref=a_all.at[rows_at],
            send_sem=ring_sem.at[0, slot], recv_sem=ring_sem.at[1, slot],
            device_id=in_plane(0, 1 if way == 0 else ts - 1), device_id_type=MESH,
        )

    hops = ts // 2
    ring = [
        [ring_copy(step, way, p) for p in range(2 if 2 * step + 2 < ts else 1) for way in range(2)]
        for step in range(hops)
    ]
    for copy in ring[0]:
        copy.start()

    rep_copies = []
    for dr in range(1, reps + 1):
        q = lax.rem(r + dr, reps)
        base = pl.multiple_of(q * block, LANE)

        def tile_left(j, _, dr=dr, base=base):
            row_copy((dr - 1) * per + j).wait()
            at = pl.ds(pl.multiple_of(base + j * tile, tile), tile)
            eh, el = split(e_mem[at, :])
            total = mul(eh, f_mem[...]) + mul(el, f_mem[...])
            part[:, at] = folded(total.T[: 2 * rank])
            return 0

        lax.fori_loop(0, per, tile_left, 0)
        if dr == 1:
            for copy in gf_copies:
                copy.wait()
            for df in range(fs):
                total = gf_slots[df * ts]
                for dt in range(1, ts):
                    total = total + gf_slots[df * ts + dt]
                gf_all[:, df * tok_g : (df + 1) * tok_g] = total
        own = stacked(gf_all[:, pl.ds(pl.multiple_of(t * tok_a, LANE), tok_a)])
        at = pl.ds(base, block)
        part[:, at] += folded(mul(own, a_ref[:, at]))
        if dr < reps:
            copy = pltpu.make_async_remote_copy(
                src_ref=part.at[:, at], dst_ref=got_rep.at[dr - 1],
                send_sem=rep_sem.at[0, dr - 1], recv_sem=rep_sem.at[1, dr - 1],
                device_id=in_sheet(dr, 0), device_id_type=MESH,
            )
            copy.start()
            rep_copies.append(copy)

    ring_waited = set()

    def forward(step):
        ready = [c for c in ring[step - 1]][: len(ring[step])]
        for i, copy in enumerate(ready):
            copy.wait_recv()
            ring_waited.add((step - 1, i))
        for copy in ring[step]:
            copy.start()

    if hops > 1:
        forward(1)
    mine = pl.ds(pl.multiple_of(r * block, LANE), block)
    total = part[:, mine]
    for i, copy in enumerate(rep_copies):
        copy.wait()
        total = total + got_rep[i]
    mid[...] = total

    cut = Cut(rank, block, ts)
    ten_copies = []
    for dt in range(1, ts):
        copy = pltpu.make_async_remote_copy(
            src_ref=mid.at[cut.at(lax.rem(t + dt, ts))], dst_ref=got_ten.at[dt - 1],
            send_sem=ten_sem.at[0, dt - 1], recv_sem=ten_sem.at[1, dt - 1],
            device_id=in_plane(0, dt), device_id_type=MESH,
        )
        copy.start()
        ten_copies.append(copy)
    total = mid[cut.at(t)]
    for i, copy in enumerate(ten_copies):
        copy.wait()
        total = total + got_ten[i]
    own = cut.at(t, r * block)
    left[own] = total * (1.0 / reps)
    back = []
    for dt in range(1, ts):
        copy = pltpu.make_async_remote_copy(
            src_ref=left.at[own], dst_ref=left.at[own],
            send_sem=ten_back.at[0, dt - 1], recv_sem=ten_back.at[1, dt - 1],
            device_id=in_plane(0, dt), device_id_type=MESH,
        )
        copy.start()
        back.append(copy)
    for copy in back:
        copy.wait()
    back = []
    for dr in range(1, reps):
        copy = pltpu.make_async_remote_copy(
            src_ref=left.at[:, mine], dst_ref=left.at[:, mine],
            send_sem=rep_back.at[0, dr - 1], recv_sem=rep_back.at[1, dr - 1],
            device_id=in_sheet(dr, 0), device_id_type=MESH,
        )
        copy.start()
        back.append(copy)
    for copy in back:
        copy.wait()

    whole = left[...]
    mix_slots[me_plane, :, 0:LANE] = jnp.zeros((rank, LANE), F32)
    mix_slots[me_plane, :, 0:rank] = mul(whole, whole, NT, HIGHEST)
    mix_slots[me_plane, :, LANE:] = folded(mul(stacked(whole), a_ref[...], NT))
    mix_copies = spread(mix_slots, mix_sem)

    n_part[...] = jnp.zeros(n_part.shape, F32)

    def tile_right(j, _):
        at = pl.ds(pl.multiple_of(j * tile, tile), tile)
        eh, el = split(e_mem[at, :])
        both = stacked(left[:, at])
        n_part[...] += folded(mul(both, eh)) + mul(both[:rank], el)
        return 0

    lax.fori_loop(0, rows // tile, tile_right, 0)

    for copy in mix_copies:
        copy.wait()
    for dt in range(ts):
        total = mix_slots[dt, :, LANE:]
        for df in range(1, fs):
            total = total + mix_slots[df * ts + dt, :, LANE:]
        al_all[:, dt * tok_a : (dt + 1) * tok_a] = total
    tokens = stacked(al_all[:, pl.ds(pl.multiple_of(f * tok_g, LANE), tok_g)])
    n_part[...] += folded(mul(tokens, g_ref[...]))

    n_cut = Cut(rank, n_part.shape[1], reps * fs)
    n_copies = []
    for i, (dr, df) in enumerate(sheet):
        owner = lax.rem(r + dr, reps) * fs + lax.rem(f + df, fs)
        copy = pltpu.make_async_remote_copy(
            src_ref=n_part.at[n_cut.at(owner)], dst_ref=n_got.at[i],
            send_sem=n_sem.at[0, i], recv_sem=n_sem.at[1, i],
            device_id=in_sheet(dr, df), device_id_type=MESH,
        )
        copy.start()
        n_copies.append(copy)

    gram = mix_slots[0, :, 0:LANE]
    for df in range(1, fs):
        gram = gram + mix_slots[df * ts, :, 0:LANE]
    inverse = inverse_factor(gram)
    high, low = split(mul(inverse, left[...], precision=HIGHEST))
    q_ref[0:rank] = high
    q_ref[rank : 2 * rank] = low
    q_ref[2 * rank :] = high

    place = n_cut.at(r * fs + f)
    total = n_part[place]
    for i, copy in enumerate(n_copies):
        copy.wait()
        total = total + n_got[i]
    n_full[place] = total * (1.0 / reps)
    back = []
    for i, (dr, df) in enumerate(sheet):
        copy = pltpu.make_async_remote_copy(
            src_ref=n_full.at[place], dst_ref=n_full.at[place],
            send_sem=n_back.at[0, i], recv_sem=n_back.at[1, i],
            device_id=in_sheet(dr, df), device_id_type=MESH,
        )
        copy.start()
        back.append(copy)
    for copy in back:
        copy.wait()
    for step in range(2, hops):
        forward(step)
    for step in range(hops):
        for i, copy in enumerate(ring[step]):
            copy.wait_send()
            if (step, i) not in ring_waited:
                copy.wait_recv()
    for copy in own_copies + g_copies:
        copy.wait()
    factor = mul(inverse, n_full[...], precision=HIGHEST)
    n_ref[...] = factor
    high, low = split(factor)
    nt_ref[0:rank] = high
    nt_ref[rank : 2 * rank] = high
    nt_ref[2 * rank :] = low


def run_front(sizes, a, g, f, e):
    reps, fs, ts = sizes
    rank, rows, columns = f.shape[0], e.shape[0], e.shape[1]
    tok_g, tok_a = g.shape[0], a.shape[0]
    block = rows // reps
    cut, n_cut = Cut(rank, block, ts), Cut(rank, columns, reps * fs)
    tiles = rows // min(256, block)
    plane, sheet = fs * ts - 1, reps * fs - 1
    vmem = pl.BlockSpec(memory_space=pltpu.VMEM)
    dma = pltpu.SemaphoreType.DMA
    return pl.pallas_call(
        functools.partial(front, sizes),
        out_shape=(
            jax.ShapeDtypeStruct((3 * rank, rows), BF16),
            jax.ShapeDtypeStruct((rank, columns), F32),
            jax.ShapeDtypeStruct((3 * rank, columns), BF16),
            pltpu.VMEM((rows, columns), F32),
            pltpu.VMEM((tok_a * ts, rows), BF16),
            pltpu.VMEM((tok_g * fs, columns), BF16),
        ),
        in_specs=[vmem, vmem, vmem, pl.BlockSpec(memory_space=pl.ANY)],
        out_specs=(vmem,) * 6,
        scratch_shapes=[
            pltpu.VMEM((columns, LANE), BF16),
            pltpu.VMEM((rank, rows), F32),
            pltpu.VMEM((rank, rows), F32),
            pltpu.VMEM((reps - 1, rank, block), F32),
            pltpu.VMEM((rank, block), F32),
            pltpu.VMEM((ts - 1, cut.rows, cut.columns), F32),
            pltpu.VMEM((fs * ts, rank, tok_g), F32),
            pltpu.VMEM((rank, tok_g * fs), F32),
            pltpu.VMEM((fs * ts, rank, LANE + tok_a), F32),
            pltpu.VMEM((rank, tok_a * ts), F32),
            pltpu.VMEM((rank, columns), F32),
            pltpu.VMEM((sheet, n_cut.rows, n_cut.columns), F32),
            pltpu.VMEM((rank, columns), F32),
            dma((tiles,)), dma((2,)), dma((2, 4 * max(1, ts // 2))), dma((2, max(1, fs - 1))), dma((2, plane)), dma((2, reps - 1)), dma((2, ts - 1)), dma((2, ts - 1)),
            dma((2, reps - 1)), dma((2, plane)), dma((2, sheet)), dma((2, sheet)),
        ],
        compiler_params=pltpu.CompilerParams(
            collective_id=0, has_side_effects=True, vmem_limit_bytes=VMEM_BYTES
        ),
        cost_estimate=pl.CostEstimate(
            flops=100_000_000_000, bytes_accessed=rows * columns * 8, transcendentals=0
        ),
        name="front",
    )(a, g, f, e)


def finish(a_ref, g_ref, e_ref, q_ref, n_ref, error_ref, update_ref):
    tile = error_ref.shape[0]
    at = pl.ds(pl.multiple_of(pl.program_id(0) * tile, tile), tile)
    low_rank = mul(q_ref[...], n_ref[...], TN)
    grad = mul(a_ref[:, at], g_ref[...], TN)
    error_ref[...] = grad + e_ref[at, :] - low_rank
    update_ref[...] = low_rank.astype(BF16)


def run_finish(a, g, e, q, n):
    rows, columns = e.shape
    tile = min(256, rows)

    def whole(x):
        return pl.BlockSpec(x.shape, lambda i: (0, 0))

    def tall(x):
        return pl.BlockSpec((x.shape[0], tile), lambda i: (0, i))

    flat = pl.BlockSpec((tile, columns), lambda i: (i, 0))
    vmem = pl.BlockSpec(memory_space=pltpu.VMEM)
    return pl.pallas_call(
        finish,
        out_shape=(jax.ShapeDtypeStruct(e.shape, F32), jax.ShapeDtypeStruct(e.shape, BF16)),
        grid=(rows // tile,),
        in_specs=[vmem, vmem, vmem, tall(q), whole(n)],
        out_specs=(flat, flat),
        compiler_params=pltpu.CompilerParams(vmem_limit_bytes=VMEM_BYTES),
        name="finish",
    )(*(pltpu.with_memory_space_constraint(x, pltpu.VMEM) for x in (a, g, e)), q, n)


def solution(mesh):
    sizes = (mesh.shape["replica"], mesh.shape["fsdp"], mesh.shape["tensor"])

    def body(attn_out, out_grad, error_in, factor_in):
        q, factor, n, held, activations, cotangents = run_front(
            sizes, attn_out, out_grad, factor_in.T, error_in[0]
        )
        new_error, update = run_finish(activations, cotangents, held, q, n)
        return new_error[None], update, factor.T

    placed = (
        P(("replica", "tensor"), "fsdp"),
        P(("replica", "fsdp"), "tensor"),
        P("replica", "fsdp", "tensor"),
        P("tensor", None),
    )
    return jax.shard_map(
        body,
        mesh=mesh,
        in_specs=placed,
        out_specs=(P("replica", "fsdp", "tensor"), P("fsdp", "tensor"), P("tensor", None)),
        check_vma=False,
    )
```

```python
import functools

import jax
import jax.numpy as jnp
from jax import lax
from jax.experimental import pallas as pl
from jax.experimental.pallas import tpu as pltpu
from jax.sharding import PartitionSpec as P

MESH = pl.DeviceIdType.MESH
HIGHEST = lax.Precision.HIGHEST
F32, BF16 = jnp.float32, jnp.bfloat16
LANE = 128
NN = (((1,), (0,)), ((), ()))
NT = (((1,), (1,)), ((), ()))
TN = (((0,), (0,)), ((), ()))
VMEM_BYTES = 20 * 1024 * 1024


def mul(a, b, dims=NN, precision=None):
    return lax.dot_general(a, b, dims, precision=precision, preferred_element_type=F32)


def split(x):
    high = x.astype(BF16)
    return high, (x - high.astype(F32)).astype(BF16)


def stacked(x):
    return jnp.concatenate(split(x), axis=0)


def folded(x):
    half = x.shape[0] // 2
    return x[:half] + x[half:]


class Cut:
    def __init__(self, rows, columns, pieces):
        self.down = 1
        while (columns * self.down) % (pieces * LANE) != 0:
            self.down *= 2
        self.across = pieces // self.down
        self.rows, self.columns = rows // self.down, columns // self.across

    def at(self, piece, start=0):
        row = pl.multiple_of((piece // self.across) * self.rows, 8)
        column = pl.multiple_of(start + (piece % self.across) * self.columns, LANE)
        return pl.ds(row, self.rows), pl.ds(column, self.columns)


def inverse_factor(gram):
    rank = gram.shape[0]
    row_at = lax.broadcasted_iota(jnp.int32, (rank, LANE), 0)
    lane_at = lax.broadcasted_iota(jnp.int32, (rank, LANE), 1)
    table = gram + jnp.where(lane_at == row_at + LANE // 2, 1.0, 0.0).astype(F32)
    for k in range(rank):
        row = table[k : k + 1, :]
        inverse = 1.0 / jnp.sqrt(row[:, k : k + 1])
        row = row * inverse
        column = jnp.where(row_at > k, table[:, k : k + 1] * inverse, 0.0)
        table = jnp.where(row_at == k, jnp.broadcast_to(row, table.shape), table - column * row)
    return table[:, LANE // 2 : LANE // 2 + rank]


def front(
    sizes,
    a_ref, g_ref, f_ref, e_ref,
    q_ref, n_ref, nt_ref, e_mem, a_all, g_all,
    f_mem, part, left, got_rep, mid, got_ten, gf_slots, gf_all, mix_slots, al_all,
    n_part, n_got, n_full,
    e_sem, own_sem, ring_sem, g_sem, gf_sem, rep_sem, ten_sem, ten_back, rep_back, mix_sem, n_sem, n_back,
):
    reps, fs, ts = sizes
    r, f, t = lax.axis_index("replica"), lax.axis_index("fsdp"), lax.axis_index("tensor")
    rank, rows = part.shape
    block = rows // reps
    tile = min(256, block)
    per = block // tile
    tok_g, tok_a = g_ref.shape[0], a_ref.shape[0]

    def row_copy(step):
        q = lax.rem(r + 1 + step // per, reps)
        at = pl.ds(pl.multiple_of(q * block + (step % per) * tile, tile), tile)
        return pltpu.make_async_copy(e_ref.at[at], e_mem.at[at], e_sem.at[step])

    for step in range(reps * per):
        row_copy(step).start()

    plane = [(df, dt) for df in range(fs) for dt in range(ts) if df + dt > 0]
    sheet = [(dr, df) for dr in range(reps) for df in range(fs) if dr + df > 0]

    def in_plane(df, dt):
        return {"replica": r, "fsdp": lax.rem(f + df, fs), "tensor": lax.rem(t + dt, ts)}

    def in_sheet(dr, df):
        return {"replica": lax.rem(r + dr, reps), "fsdp": lax.rem(f + df, fs), "tensor": t}

    barrier = pltpu.get_barrier_semaphore()
    greeted = [in_plane(*d) for d in plane] + [in_sheet(*d) for d in sheet if d[0] > 0]
    for device in greeted:
        pl.semaphore_signal(barrier, inc=1, device_id=device, device_id_type=MESH)

    high, low = split(f_ref[...])
    wide = jnp.concatenate(
        [high.astype(F32), low.astype(F32), jnp.zeros((LANE - 2 * rank, f_ref.shape[1]), F32)], axis=0
    )
    f_mem[...] = wide.T.astype(BF16)

    me_plane = f * ts + t
    gf_slots[me_plane] = folded(mul(g_ref[...], f_mem[...]).T[: 2 * rank])
    pl.semaphore_wait(barrier, len(greeted))

    def spread(slots, sems):
        copies = []
        for i, d in enumerate(plane):
            copies.append(pltpu.make_async_remote_copy(
                src_ref=slots.at[me_plane], dst_ref=slots.at[me_plane],
                send_sem=sems.at[0, i], recv_sem=sems.at[1, i],
                device_id=in_plane(*d), device_id_type=MESH,
            ))
            copies[-1].start()
        return copies

    gf_copies = spread(gf_slots, gf_sem)

    g_own = pl.ds(pl.multiple_of(f * tok_g, tok_g), tok_g)
    a_own = pl.ds(pl.multiple_of(t * tok_a, tok_a), tok_a)
    own_copies = [
        pltpu.make_async_copy(a_ref, a_all.at[a_own], own_sem.at[0]),
        pltpu.make_async_copy(g_ref, g_all.at[g_own], own_sem.at[1]),
    ]
    for copy in own_copies:
        copy.start()
    g_copies = []
    for df in range(1, fs):
        copy = pltpu.make_async_remote_copy(
            src_ref=g_ref, dst_ref=g_all.at[g_own],
            send_sem=g_sem.at[0, df - 1], recv_sem=g_sem.at[1, df - 1],
            device_id=in_plane(df, 0), device_id_type=MESH,
        )
        copy.start()
        g_copies.append(copy)

    pieces = 4
    piece = tok_a // pieces

    def rows_of(block_at, p):
        return pl.ds(pl.multiple_of(block_at * tok_a + p * piece, piece), piece)

    def inside(x):
        return jnp.logical_and(x >= 0, x < ts)

    def bulk(way, d, p):
        sign = 1 - 2 * way
        block_at = t if d <= 2 else t - sign * (d - 1)
        dest = t + sign * (d if d <= 2 else 1)
        held = lax.rem(block_at + ts, ts)
        src = a_ref.at[pl.ds(p * piece, piece)] if d <= 2 else a_all.at[rows_of(held, p)]
        slot = (way * (ts - 1) + d - 1) * pieces + p
        copy = pltpu.make_async_remote_copy(
            src_ref=src, dst_ref=a_all.at[rows_of(held, p)],
            send_sem=ring_sem.at[0, slot], recv_sem=ring_sem.at[1, slot],
            device_id={"replica": r, "fsdp": f, "tensor": lax.rem(dest + ts, ts)},
            device_id_type=MESH,
        )
        return copy, jnp.logical_and(inside(block_at), inside(dest))

    started, landed = [], set()

    def send(d, p):
        if d >= ts:
            return
        for way in range(2):
            copy, valid = bulk(way, d, p)
            pl.when(valid)(copy.start)
            started.append((copy, valid))

    def land(d, p):
        if d >= ts or (d, p) in landed:
            return
        landed.add((d, p))
        for way in range(2):
            sign = 1 - 2 * way
            block_at = t - sign * d
            at = a_all.at[rows_of(lax.rem(block_at + ts, ts), p)]
            slot = (way * (ts - 1) + d - 1) * pieces + p
            copy = pltpu.make_async_remote_copy(
                src_ref=at, dst_ref=at, send_sem=ring_sem.at[0, slot], recv_sem=ring_sem.at[1, slot],
                device_id=in_plane(0, 1), device_id_type=MESH,
            )
            pl.when(inside(block_at))(copy.wait_recv)

    def pass_on(p):
        if ts > 3:
            land(2, p)
            send(3, p)

    send(2, 0)
    send(2, 1)
    send(1, 0)

    rep_copies = []
    for dr in range(1, reps + 1):
        q = lax.rem(r + dr, reps)
        base = pl.multiple_of(q * block, LANE)

        def tile_left(j, _, dr=dr, base=base):
            row_copy((dr - 1) * per + j).wait()
            at = pl.ds(pl.multiple_of(base + j * tile, tile), tile)
            eh, el = split(e_mem[at, :])
            total = mul(eh, f_mem[...]) + mul(el, f_mem[...])
            part[:, at] = folded(total.T[: 2 * rank])
            return 0

        lax.fori_loop(0, per, tile_left, 0)
        if dr == 1:
            for copy in gf_copies:
                copy.wait()
            for df in range(fs):
                total = gf_slots[df * ts]
                for dt in range(1, ts):
                    total = total + gf_slots[df * ts + dt]
                gf_all[:, df * tok_g : (df + 1) * tok_g] = total
        own = stacked(gf_all[:, pl.ds(pl.multiple_of(t * tok_a, LANE), tok_a)])
        at = pl.ds(base, block)
        part[:, at] += folded(mul(own, a_ref[:, at]))
        if dr < reps:
            copy = pltpu.make_async_remote_copy(
                src_ref=part.at[:, at], dst_ref=got_rep.at[dr - 1],
                send_sem=rep_sem.at[0, dr - 1], recv_sem=rep_sem.at[1, dr - 1],
                device_id=in_sheet(dr, 0), device_id_type=MESH,
            )
            copy.start()
            rep_copies.append(copy)

    mine = pl.ds(pl.multiple_of(r * block, LANE), block)
    total = part[:, mine]
    for i, copy in enumerate(rep_copies):
        copy.wait()
        total = total + got_rep[i]
    mid[...] = total

    cut = Cut(rank, block, ts)
    ten_copies = []
    for dt in range(1, ts):
        copy = pltpu.make_async_remote_copy(
            src_ref=mid.at[cut.at(lax.rem(t + dt, ts))], dst_ref=got_ten.at[dt - 1],
            send_sem=ten_sem.at[0, dt - 1], recv_sem=ten_sem.at[1, dt - 1],
            device_id=in_plane(0, dt), device_id_type=MESH,
        )
        copy.start()
        ten_copies.append(copy)
    total = mid[cut.at(t)]
    for i, copy in enumerate(ten_copies):
        copy.wait()
        total = total + got_ten[i]
    own = cut.at(t, r * block)
    left[own] = total * (1.0 / reps)
    back = []
    for dt in range(1, ts):
        copy = pltpu.make_async_remote_copy(
            src_ref=left.at[own], dst_ref=left.at[own],
            send_sem=ten_back.at[0, dt - 1], recv_sem=ten_back.at[1, dt - 1],
            device_id=in_plane(0, dt), device_id_type=MESH,
        )
        copy.start()
        back.append(copy)
    for copy in back:
        copy.wait()
    send(2, 2)
    pass_on(0)
    pass_on(1)
    back = []
    for dr in range(1, reps):
        copy = pltpu.make_async_remote_copy(
            src_ref=left.at[:, mine], dst_ref=left.at[:, mine],
            send_sem=rep_back.at[0, dr - 1], recv_sem=rep_back.at[1, dr - 1],
            device_id=in_sheet(dr, 0), device_id_type=MESH,
        )
        copy.start()
        back.append(copy)
    for copy in back:
        copy.wait()

    whole = left[...]
    mix_slots[me_plane, :, 0:LANE] = jnp.zeros((rank, LANE), F32)
    mix_slots[me_plane, :, 0:rank] = mul(whole, whole, NT, HIGHEST)
    mix_slots[me_plane, :, LANE:] = folded(mul(stacked(whole), a_ref[...], NT))
    mix_copies = spread(mix_slots, mix_sem)
    send(2, 3)
    for p in range(1, pieces):
        send(1, p)

    n_part[...] = jnp.zeros(n_part.shape, F32)

    def tile_right(j, _):
        at = pl.ds(pl.multiple_of(j * tile, tile), tile)
        eh, el = split(e_mem[at, :])
        both = stacked(left[:, at])
        n_part[...] += folded(mul(both, eh)) + mul(both[:rank], el)
        return 0

    lax.fori_loop(0, rows // tile, tile_right, 0)

    for copy in mix_copies:
        copy.wait()
    pass_on(2)
    for dt in range(ts):
        total = mix_slots[dt, :, LANE:]
        for df in range(1, fs):
            total = total + mix_slots[df * ts + dt, :, LANE:]
        al_all[:, dt * tok_a : (dt + 1) * tok_a] = total
    tokens = stacked(al_all[:, pl.ds(pl.multiple_of(f * tok_g, LANE), tok_g)])
    n_part[...] += folded(mul(tokens, g_ref[...]))

    n_cut = Cut(rank, n_part.shape[1], reps * fs)
    n_copies = []
    for i, (dr, df) in enumerate(sheet):
        owner = lax.rem(r + dr, reps) * fs + lax.rem(f + df, fs)
        copy = pltpu.make_async_remote_copy(
            src_ref=n_part.at[n_cut.at(owner)], dst_ref=n_got.at[i],
            send_sem=n_sem.at[0, i], recv_sem=n_sem.at[1, i],
            device_id=in_sheet(dr, df), device_id_type=MESH,
        )
        copy.start()
        n_copies.append(copy)

    gram = mix_slots[0, :, 0:LANE]
    for df in range(1, fs):
        gram = gram + mix_slots[df * ts, :, 0:LANE]
    inverse = inverse_factor(gram)
    high, low = split(mul(inverse, left[...], precision=HIGHEST))
    q_ref[0:rank] = high
    q_ref[rank : 2 * rank] = low
    q_ref[2 * rank :] = high

    place = n_cut.at(r * fs + f)
    total = n_part[place]
    for i, copy in enumerate(n_copies):
        copy.wait()
        total = total + n_got[i]
    n_full[place] = total * (1.0 / reps)
    back = []
    for i, (dr, df) in enumerate(sheet):
        copy = pltpu.make_async_remote_copy(
            src_ref=n_full.at[place], dst_ref=n_full.at[place],
            send_sem=n_back.at[0, i], recv_sem=n_back.at[1, i],
            device_id=in_sheet(dr, df), device_id_type=MESH,
        )
        copy.start()
        back.append(copy)
    for copy in back:
        copy.wait()
    pass_on(3)
    for d in range(4, ts):
        for p in range(pieces):
            land(d - 1, p)
            send(d, p)
    for d in range(1, ts):
        for p in range(pieces):
            land(d, p)
    for copy, valid in started:
        pl.when(valid)(copy.wait_send)
    for copy in own_copies + g_copies:
        copy.wait()
    factor = mul(inverse, n_full[...], precision=HIGHEST)
    n_ref[...] = factor
    high, low = split(factor)
    nt_ref[0:rank] = high
    nt_ref[rank : 2 * rank] = high
    nt_ref[2 * rank :] = low


def run_front(sizes, a, g, f, e):
    reps, fs, ts = sizes
    rank, rows, columns = f.shape[0], e.shape[0], e.shape[1]
    tok_g, tok_a = g.shape[0], a.shape[0]
    block = rows // reps
    cut, n_cut = Cut(rank, block, ts), Cut(rank, columns, reps * fs)
    tiles = rows // min(256, block)
    plane, sheet = fs * ts - 1, reps * fs - 1
    vmem = pl.BlockSpec(memory_space=pltpu.VMEM)
    dma = pltpu.SemaphoreType.DMA
    return pl.pallas_call(
        functools.partial(front, sizes),
        out_shape=(
            jax.ShapeDtypeStruct((3 * rank, rows), BF16),
            jax.ShapeDtypeStruct((rank, columns), F32),
            jax.ShapeDtypeStruct((3 * rank, columns), BF16),
            pltpu.VMEM((rows, columns), F32),
            pltpu.VMEM((tok_a * ts, rows), BF16),
            pltpu.VMEM((tok_g * fs, columns), BF16),
        ),
        in_specs=[vmem, vmem, vmem, pl.BlockSpec(memory_space=pl.ANY)],
        out_specs=(vmem,) * 6,
        scratch_shapes=[
            pltpu.VMEM((columns, LANE), BF16),
            pltpu.VMEM((rank, rows), F32),
            pltpu.VMEM((rank, rows), F32),
            pltpu.VMEM((reps - 1, rank, block), F32),
            pltpu.VMEM((rank, block), F32),
            pltpu.VMEM((ts - 1, cut.rows, cut.columns), F32),
            pltpu.VMEM((fs * ts, rank, tok_g), F32),
            pltpu.VMEM((rank, tok_g * fs), F32),
            pltpu.VMEM((fs * ts, rank, LANE + tok_a), F32),
            pltpu.VMEM((rank, tok_a * ts), F32),
            pltpu.VMEM((rank, columns), F32),
            pltpu.VMEM((sheet, n_cut.rows, n_cut.columns), F32),
            pltpu.VMEM((rank, columns), F32),
            dma((tiles,)), dma((2,)), dma((2, 8 * max(1, ts - 1))), dma((2, max(1, fs - 1))), dma((2, plane)), dma((2, reps - 1)), dma((2, ts - 1)), dma((2, ts - 1)),
            dma((2, reps - 1)), dma((2, plane)), dma((2, sheet)), dma((2, sheet)),
        ],
        compiler_params=pltpu.CompilerParams(
            collective_id=0, has_side_effects=True, vmem_limit_bytes=VMEM_BYTES
        ),
        cost_estimate=pl.CostEstimate(
            flops=100_000_000_000, bytes_accessed=rows * columns * 8, transcendentals=0
        ),
        name="front",
    )(a, g, f, e)


def finish(a_ref, g_ref, e_ref, q_ref, n_ref, error_ref, update_ref):
    tile = error_ref.shape[0]
    at = pl.ds(pl.multiple_of(pl.program_id(0) * tile, tile), tile)
    low_rank = mul(q_ref[...], n_ref[...], TN)
    grad = mul(a_ref[:, at], g_ref[...], TN)
    error_ref[...] = grad + e_ref[at, :] - low_rank
    update_ref[...] = low_rank.astype(BF16)


def run_finish(a, g, e, q, n):
    rows, columns = e.shape
    tile = min(256, rows)

    def whole(x):
        return pl.BlockSpec(x.shape, lambda i: (0, 0))

    def tall(x):
        return pl.BlockSpec((x.shape[0], tile), lambda i: (0, i))

    flat = pl.BlockSpec((tile, columns), lambda i: (i, 0))
    vmem = pl.BlockSpec(memory_space=pltpu.VMEM)
    return pl.pallas_call(
        finish,
        out_shape=(jax.ShapeDtypeStruct(e.shape, F32), jax.ShapeDtypeStruct(e.shape, BF16)),
        grid=(rows // tile,),
        in_specs=[vmem, vmem, vmem, tall(q), whole(n)],
        out_specs=(flat, flat),
        compiler_params=pltpu.CompilerParams(vmem_limit_bytes=VMEM_BYTES),
        name="finish",
    )(*(pltpu.with_memory_space_constraint(x, pltpu.VMEM) for x in (a, g, e)), q, n)


def solution(mesh):
    sizes = (mesh.shape["replica"], mesh.shape["fsdp"], mesh.shape["tensor"])

    def body(attn_out, out_grad, error_in, factor_in):
        q, factor, n, held, activations, cotangents = run_front(
            sizes, attn_out, out_grad, factor_in.T, error_in[0]
        )
        new_error, update = run_finish(activations, cotangents, held, q, n)
        return new_error[None], update, factor.T

    placed = (
        P(("replica", "tensor"), "fsdp"),
        P(("replica", "fsdp"), "tensor"),
        P("replica", "fsdp", "tensor"),
        P("tensor", None),
    )
    return jax.shard_map(
        body,
        mesh=mesh,
        in_specs=placed,
        out_specs=(P("replica", "fsdp", "tensor"), P("fsdp", "tensor"), P("tensor", None)),
        check_vma=False,
    )
```
